32 devices in a mesh: gx: 4 (over y, x), gy: 8 (over z, core).
Axes of the slice: x: 2, y: 2, z: 4, core: 2. Of those that a mesh axis runs over, the one named last changes fastest.
Arguments:
- surface: float32 [256, 4096], P('gx', 'gy'), may hold values from -6 to 6
- east_velocity: float32 [256, 4096], P('gx', 'gy'), may hold values from -3 to 3
- north_velocity: float32 [256, 4096], P('gx', 'gy'), may hold values from -3 to 3
- east_depth: float32 [256, 4096], P('gx', 'gy'), may hold values from 0.25 to 2
- north_depth: float32 [256, 4096], P('gx', 'gy'), may hold values from 0.25 to 2
- slot_gauge: int32 [32, 128], P(('gx', 'gy')), may hold values from 0 to 2048, as said below
- slot_cell: int32 [32, 128], P(('gx', 'gy')), may hold values from 0 to 32767
Outputs:
- final_surface: float32 [256, 4096], P('gx', 'gy')
- final_east: float32 [256, 4096], P('gx', 'gy')
- final_north: float32 [256, 4096], P('gx', 'gy')
- gauge_series: float32 [2048, 48], P(('gx', 'gy'))
The draws below stay inside these ranges and needn't reach their ends.
Inputs may be any that keep to these rules, and one draw needn't show every extreme that they name: `slot_gauge`: entries below 2048 are gauge ids: every id 0 to 2047 stands exactly once in the whole array, in the row of the device whose block holds that gauge; the ids owned by device d, d * 64 to (d + 1) * 64 - 1, all lie in blocks with d's gx index. Each row lists its ids first, then 2048 in the unused slots. Some device's row is full in every draw.
All inputs are finite; a program needn't handle non-finite values.
Results may differ from the reference program's by a relative error of at most 0.00012.
Values sent between devices are 32-bit elements; how exact they have to be, the bound alone decides.
A program may use at most 64 MiB of HBM per device.

```python
import math
import jax
import jax.numpy as jnp

CX = 64
CY = 512
STEPS = 16
SLOTS = 128
GAUGE_DEV = 64
NX = 256
NY = 4096
GAUGES = 2048
N_GX = 4
N_GY = 8
DEVICES = 32


def draw_slot_gauge(key, part):
    base = jax.random.fold_in(key, 11)
    key_weight, key_busy, key_perm = jax.random.split(base, 3)
    weights = jax.random.randint(key_weight, (N_GX, N_GY), 1, 3)
    busy = jax.random.randint(key_busy, (N_GX,), 0, N_GY)
    column = jnp.arange(N_GY, dtype=jnp.int32)
    is_busy = column[None, :] == busy[:, None]
    weights = jnp.where(is_busy, 0, weights)
    remain = N_GY * GAUGE_DEV - SLOTS
    cumul = jnp.cumsum(weights, axis=1)
    ends = remain * cumul // cumul[:, -1:]
    counts = ends - jnp.concatenate([jnp.zeros((N_GX, 1), jnp.int32), ends[:, :-1]], 1)
    counts = jnp.where(is_busy, SLOTS, counts)
    starts = jnp.cumsum(counts, axis=1) - counts
    band = N_GY * GAUGE_DEV
    perms = jax.vmap(lambda sub: jax.random.permutation(sub, band))(jax.random.split(key_perm, N_GX))
    slot = jnp.arange(SLOTS, dtype=jnp.int32)
    position = jnp.minimum(starts[:, :, None] + slot[None, None, :], band - 1)
    spread = jnp.broadcast_to(perms[:, None, :], (N_GX, N_GY, band))
    picked = jnp.take_along_axis(spread, position, axis=2)
    gauge_ids = jnp.arange(N_GX, dtype=jnp.int32)[:, None, None] * band + picked
    valid = slot[None, None, :] < counts[:, :, None]
    return jnp.where(valid, gauge_ids, GAUGES).reshape(N_GX * N_GY, SLOTS).astype(jnp.int32)


def draw_surface(key, part):
    key_rough = jax.random.fold_in(jax.random.fold_in(key, 23), 0)
    rough = jax.random.normal(key_rough, (NX, NY), jnp.float32)
    return jnp.clip(rough, -6.0, 6.0)


def plant(entries, key, least, top_value):
    shape = entries.shape
    place = [jax.random.randint(jax.random.fold_in(key, axis), (), 0, shape[axis]) for axis in range(len(shape))]
    entries = entries.at[tuple(place)].set(least)
    longest = shape.index(max(shape))
    place[longest] = (place[longest] + 1) % shape[longest]
    return entries.at[tuple(place)].set(top_value)


def shard_levels(key, extent, shards, low, high):
    level, own = 1.0, jax.random.fold_in(key, 6)
    for axis_at, blocks in shards:
        draws = jnp.exp(jax.random.uniform(jax.random.fold_in(own, axis_at), (blocks,), jnp.float32, low / len(shards), high / len(shards)))
        level = level * jnp.repeat(draws, extent[axis_at] // blocks).reshape([-1 if axis == axis_at else 1 for axis in range(len(extent))])
    return level


def bell_draw(rng, extent, deviation, most, cuts=(), kind=jnp.bfloat16):
    values = deviation * jax.random.normal(rng, extent, jnp.float32)
    if cuts:
        values = values * shard_levels(rng, extent, cuts, -0.22, 0.18)
    return jnp.clip(values, -most, most).astype(kind)


def setup_inputs(seed: int = 0) -> dict:
    keys = jax.random.split(jax.random.key(seed), 8)
    return {
        "surface": draw_surface(jax.random.fold_in(keys[7], 71), 0),
        "east_velocity": bell_draw(keys[1], (NX, NY), 0.5, 3.0, ((0, 4), (1, 8)), jnp.float32),
        "north_velocity": bell_draw(keys[2], (NX, NY), 0.5, 3.0, ((0, 4), (1, 8)), jnp.float32),
        "east_depth": jnp.clip(jnp.exp(math.log(2.0) - 2.0794415 * jax.random.uniform(keys[3], (NX, NY), jnp.float32) ** shard_levels(keys[3], (NX, NY), ((0, 4), (1, 8)), -0.2, 0.2)), 0.25, 2.0),
        "north_depth": jnp.clip(jnp.exp(math.log(2.0) - 2.0794415 * jax.random.uniform(keys[4], (NX, NY), jnp.float32) ** shard_levels(keys[4], (NX, NY), ((0, 4), (1, 8)), -0.2, 0.2)), 0.25, 2.0),
        "slot_gauge": draw_slot_gauge(jax.random.fold_in(keys[7], 71), 0),
        "slot_cell": plant(jax.random.randint(keys[6], (DEVICES, SLOTS), 0, CX * CY), jax.random.fold_in(keys[6], 1), 0, (CX * CY) - 1).astype(jnp.int32),
    }


time_step = 0.45


def advance(eta, east, north, east_depth, north_depth):
    eta_down = jnp.concatenate([eta[1:], jnp.zeros_like(eta[:1])], 0)
    eta_right = jnp.concatenate([eta[:, 1:], jnp.zeros_like(eta[:, :1])], 1)
    east = east - time_step * (eta_down - eta)
    north = north - time_step * (eta_right - eta)
    flux_x = east_depth * east
    flux_y = north_depth * north
    flux_up = jnp.concatenate([jnp.zeros_like(flux_x[:1]), flux_x[:-1]], 0)
    flux_left = jnp.concatenate([jnp.zeros_like(flux_y[:, :1]), flux_y[:, :-1]], 1)
    eta = eta - time_step * (flux_x - flux_up + flux_y - flux_left)
    return eta, east, north


def reference(surface, east_velocity, north_velocity, east_depth, north_depth, slot_gauge, slot_cell):
    device = jnp.arange(slot_gauge.shape[0], dtype=jnp.int32)[:, None]
    grid_rows = ((device // N_GY) * CX + slot_cell // CY).reshape(-1).astype(jnp.int32)
    grid_cols = ((device % N_GY) * CY + slot_cell % CY).reshape(-1).astype(jnp.int32)
    eta, east, north = surface, east_velocity, north_velocity
    records = []
    for step in range(STEPS):
        eta, east, north = advance(eta, east, north, east_depth, north_depth)
        records.append(jnp.stack([eta[grid_rows, grid_cols], east[grid_rows, grid_cols], north[grid_rows, grid_cols]]))
    stacked = jnp.stack(records)
    flat = jnp.transpose(stacked, (2, 1, 0)).reshape(grid_rows.shape[0], 3 * STEPS)
    holder = jnp.zeros((GAUGES + 1, 3 * STEPS), flat.dtype)
    series = holder.at[slot_gauge.reshape(-1).astype(jnp.int32)].set(flat)[:GAUGES]
    return eta, east, north, series
```

```python
import jax
import jax.numpy as jnp
from jax import lax
from jax.experimental import pallas as pl
from jax.experimental.pallas import tpu as pltpu
from jax.sharding import PartitionSpec as P

STEPS = 16
GAUGE_DEV = 64
LANES = 128
HALO = STEPS
time_step = 0.45
MESH = pl.DeviceIdType.MESH


def kernel(
    n_gx, n_gy, eta_hbm, east_hbm, north_hbm, hx_hbm, hy_hbm, ids_ref, cell_ref,
    eta_out, east_out, north_out, series_out,
    wide, hist, packed, sides, final_eta, outbox, inbox, series_buf,
    load_sem, row_send, row_recv, col_send, col_recv, corner_send, corner_recv,
    mail_send, mail_recv, out_sem,
):
    rows, cols = eta_hbm.shape
    chunks = cols // LANES
    tall = rows + 2 * HALO
    plane = (chunks + 1) * tall
    a, b = lax.axis_index("gx"), lax.axis_index("gy")
    has_up, has_down = a > 0, a < n_gx - 1
    has_left, has_right = b > 0, b < n_gy - 1

    loads = []
    for f, src in enumerate((eta_hbm, east_hbm, north_hbm, hx_hbm, hy_hbm)):
        for c in range(chunks):
            copy = pltpu.make_async_copy(
                src.at[:, c * LANES:(c + 1) * LANES],
                wide.at[f, c, HALO:HALO + rows, :], load_sem.at[f, c])
            copy.start()
            loads.append(copy)

    zero_rows = jnp.zeros((5, chunks, HALO, LANES), jnp.float32)
    zero_side = jnp.zeros((tall, LANES), jnp.float32)
    zero_cap = jnp.zeros((2, HALO, LANES), jnp.float32)

    @pl.when(jnp.logical_not(has_up))
    def _():
        wide[:, 0:chunks, 0:HALO, :] = zero_rows
        sides[:, 0:HALO, :] = zero_cap

    @pl.when(jnp.logical_not(has_down))
    def _():
        wide[:, 0:chunks, HALO + rows:tall, :] = zero_rows
        sides[:, HALO + rows:tall, :] = zero_cap

    @pl.when(jnp.logical_not(has_left))
    def _():
        sides[0, HALO:HALO + rows, :] = zero_side[:rows]

    @pl.when(jnp.logical_not(has_right))
    def _():
        sides[1, HALO:HALO + rows, :] = zero_side[:rows]

    barrier = pltpu.get_barrier_semaphore()

    @pl.when(has_up)
    def _():
        pl.semaphore_signal(barrier, inc=1, device_id=(a - 1, b), device_id_type=MESH)

    @pl.when(has_down)
    def _():
        pl.semaphore_signal(barrier, inc=1, device_id=(a + 1, b), device_id_type=MESH)

    for d in range(1, n_gy):
        pl.semaphore_signal(barrier, inc=1, device_id=(a, lax.rem(b + d, n_gy)), device_id_type=MESH)
    pl.semaphore_wait(
        barrier, n_gy - 1 + has_up.astype(jnp.int32) + has_down.astype(jnp.int32))

    for copy in loads:
        copy.wait()

    def row_copy(k):
        source = (HALO, rows)[k]
        target = (HALO + rows, 0)[k]
        return pltpu.make_async_remote_copy(
            wide.at[:, 0:chunks, source:source + HALO, :],
            wide.at[:, 0:chunks, target:target + HALO, :],
            row_send.at[k], row_recv.at[k],
            device_id=(a + (-1, 1)[k], b), device_id_type=MESH)

    def corner_copy(k):
        source = (HALO, rows)[k]
        target = (HALO + rows, 0)[k]
        return pltpu.make_async_remote_copy(
            sides.at[:, source:source + HALO, :], sides.at[:, target:target + HALO, :],
            corner_send.at[k], corner_recv.at[k],
            device_id=(a + (-1, 1)[k], b), device_id_type=MESH)

    def col_copy(k):
        return pltpu.make_async_remote_copy(
            packed.at[k], sides.at[k, HALO:HALO + rows, :],
            col_send.at[k], col_recv.at[k],
            device_id=(a, b + (1, -1)[k]), device_id_type=MESH)

    lane = lax.broadcasted_iota(jnp.int32, (rows, LANES), 1)
    for k in range(2):
        total = jnp.zeros((rows, LANES), jnp.float32)
        for f in range(5):
            tile = wide[f, (chunks - 1, 0)[k], HALO:HALO + rows, :]
            shift = (f * HALO + (HALO, 0)[k]) % LANES
            moved = pltpu.roll(tile, shift, axis=1) if shift else tile
            total = jnp.where((lane >= f * HALO) & (lane < (f + 1) * HALO), moved, total)
        packed[k] = total

    @pl.when(has_right)
    def _():
        col_copy(0).start()

    @pl.when(has_left)
    def _():
        col_copy(1).start()

    @pl.when(has_up)
    def _():
        row_copy(0).start()

    @pl.when(has_down)
    def _():
        row_copy(1).start()

    @pl.when(has_right)
    def _():
        col_copy(0).wait_send()
        col_copy(1).wait_recv()

    @pl.when(has_left)
    def _():
        col_copy(1).wait_send()
        col_copy(0).wait_recv()

    @pl.when(has_up)
    def _():
        corner_copy(0).start()

    @pl.when(has_down)
    def _():
        corner_copy(1).start()

    @pl.when(has_up)
    def _():
        row_copy(0).wait_send()
        row_copy(1).wait_recv()
        corner_copy(0).wait_send()
        corner_copy(1).wait_recv()

    @pl.when(has_down)
    def _():
        row_copy(1).wait_send()
        row_copy(0).wait_recv()
        corner_copy(1).wait_send()
        corner_copy(0).wait_recv()

    lane = lax.broadcasted_iota(jnp.int32, (tall, LANES), 1)
    scales = (time_step, 1.0, 1.0, time_step * time_step, time_step * time_step)
    for f in range(5):
        for c in range(chunks + 1):
            if c < chunks:
                tile = wide[f, c]
            else:
                left, right = sides[0], sides[1]
                left = pltpu.roll(left, (LANES - HALO - f * HALO) % LANES, axis=1)
                if f:
                    right = pltpu.roll(right, (LANES - f * HALO) % LANES, axis=1)
                tile = jnp.where(lane < HALO, right, jnp.where(lane >= LANES - HALO, left, 0.0))
            if f in (0, 3, 4):
                tile = tile * scales[f]
            if f < 3:
                start = f * (STEPS + 1) * plane + c * tall
                hist[start:start + tall, :] = tile
            else:
                wide[f, c] = tile

    keep_row = has_down.astype(jnp.float32)
    keep_col = has_right.astype(jnp.float32)
    first_lane, last_lane = lane == 0, lane == LANES - 1
    side_mask = jnp.where(lane < LANES // 2, keep_col, 1.0)

    def step(s, carry):
        def at(f, c, t):
            return pl.ds(pl.multiple_of((f * (STEPS + 1) + t) * plane + c * tall, 8), tall)

        def put_eta(c, new):
            base = pl.multiple_of((s + 1) * plane + c * tall, 8)
            if c == chunks:
                new = new * side_mask
            hist[pl.ds(base, HALO + rows), :] = new[:HALO + rows]
            hist[pl.ds(base + HALO + rows, HALO), :] = new[HALO + rows:] * keep_row

        def rolled_eta(c):
            return pltpu.roll(hist[at(0, c, s), :], LANES - 1, axis=1)

        order = [chunks] + list(range(chunks))
        rolled = rolled_eta(chunks)
        held = None
        behind = None
        for c in order:
            after = rolled_eta((c + 1) % (chunks + 1))
            eta = hist[at(0, c, s), :]
            east = hist[at(1, c, s), :] - (pltpu.roll(eta, tall - 1, axis=0) - eta)
            north = hist[at(2, c, s), :] - (jnp.where(last_lane, after, rolled) - eta)
            hist[at(1, c, s + 1), :] = east
            hist[at(2, c, s + 1), :] = north
            fx = wide[3, c] * east
            fy = wide[4, c] * north
            part = eta - (fx - pltpu.roll(fx, 1, axis=0)) - fy
            moved = pltpu.roll(fy, 1, axis=1)
            if c == chunks:
                held = (part, moved)
            else:
                put_eta(c, part + jnp.where(first_lane, behind, moved))
            behind = moved
            rolled = after
        part, moved = held
        put_eta(chunks, part + jnp.where(first_lane, behind, moved))
        return carry

    lax.fori_loop(0, STEPS, step, 0)

    outs = []
    for c in range(chunks):
        start = STEPS * plane + c * tall + HALO
        final_eta[c] = hist[start:start + rows, :] * (1.0 / time_step)
        where_out = pl.ds(c * LANES, LANES)
        outs.append(pltpu.make_async_copy(final_eta.at[c], eta_out.at[:, where_out], out_sem.at[0, c]))
        for f, dst in ((1, east_out), (2, north_out)):
            start = (f * (STEPS + 1) + STEPS) * plane + c * tall + HALO
            outs.append(pltpu.make_async_copy(
                hist.at[start:start + rows, :], dst.at[:, where_out], out_sem.at[f, c]))
    for copy in outs:
        copy.start()

    slots = ids_ref.shape[1]
    slot_lane = lax.broadcasted_iota(jnp.int32, (STEPS, slots), 1)

    def pick(k, kept):
        cell = cell_ref[0, k]
        row = cell // cols
        col = cell - row * cols
        chunk = col // LANES
        here = col - chunk * LANES
        start = plane + chunk * tall + HALO + row
        shift = lax.rem(k - here + LANES, LANES)
        new = []
        for f in range(3):
            slab = hist[pl.ds(f * (STEPS + 1) * plane + start, STEPS, stride=plane), :]
            slab = pltpu.roll(slab, shift, axis=1)
            new.append(jnp.where(slot_lane == k, slab, kept[f]))
        return tuple(new)

    blank = jnp.zeros((STEPS, slots), jnp.float32)
    kept = lax.fori_loop(0, slots, pick, (blank, blank, blank), unroll=8)
    records = jnp.concatenate([kept[0] * (1.0 / time_step), kept[1], kept[2]], 0)
    half = 3 * STEPS // 2
    pair = jnp.concatenate([records[:half], records[half:]], 1)
    high = pair.astype(jnp.bfloat16)
    rest = pair - high.astype(jnp.float32)
    middle = rest.astype(jnp.bfloat16)
    low = (rest - middle.astype(jnp.float32)).astype(jnp.bfloat16)
    local_ids = ids_ref[...] - a * (n_gy * GAUGE_DEV)
    entry = lax.broadcasted_iota(jnp.int32, (2 * GAUGE_DEV, slots), 0)
    for o in range(n_gy):
        lower = (entry < GAUGE_DEV) & (local_ids == entry + o * GAUGE_DEV)
        upper = (entry >= GAUGE_DEV) & (local_ids == entry + (o - 1) * GAUGE_DEV)
        chooser = jnp.concatenate(
            [jnp.where(lower, 1.0, 0.0), jnp.where(upper, 1.0, 0.0)], 1).astype(jnp.bfloat16)
        total = None
        for piece in (low, middle, high):
            got = lax.dot_general(piece, chooser, (((1,), (1,)), ((), ())),
                                  preferred_element_type=jnp.float32)
            total = got if total is None else total + got
        outbox[o] = total

    def mail(d):
        peer = lax.rem(b + d, n_gy)
        return pltpu.make_async_remote_copy(
            outbox.at[peer], inbox.at[d], mail_send.at[d], mail_recv.at[d],
            device_id=(a, peer), device_id_type=MESH)

    for d in range(1, n_gy):
        mail(d).start()
    total = outbox[b]
    for d in range(1, n_gy):
        mail(d).wait_recv()
        total = total + inbox[d]
    flipped = total.T
    series_buf[:, 0:half] = flipped[:GAUGE_DEV]
    series_buf[:, half:2 * half] = flipped[GAUGE_DEV:]
    last = pltpu.make_async_copy(series_buf, series_out, out_sem.at[0, chunks])
    last.start()
    for d in range(1, n_gy):
        mail(d).wait_send()
    for copy in outs:
        copy.wait()
    last.wait()


def solution(mesh):
    n_gx, n_gy = mesh.shape["gx"], mesh.shape["gy"]

    def shards(surface, east_velocity, north_velocity, east_depth, north_depth, slot_gauge, slot_cell):
        rows, cols = surface.shape
        chunks = cols // LANES
        tall = rows + 2 * HALO
        plane = (chunks + 1) * tall
        half = 3 * STEPS // 2
        field = jax.ShapeDtypeStruct((rows, cols), jnp.float32)
        anywhere = pl.BlockSpec(memory_space=pl.ANY)
        dma = pltpu.SemaphoreType.DMA
        return pl.pallas_call(
            lambda *refs: kernel(n_gx, n_gy, *refs),
            name="window",
            out_shape=(field, field, field,
                       jax.ShapeDtypeStruct((GAUGE_DEV, 3 * STEPS), jnp.float32)),
            in_specs=[anywhere] * 5 + [pl.BlockSpec(memory_space=pltpu.VMEM),
                                       pl.BlockSpec(memory_space=pltpu.SMEM)],
            out_specs=(anywhere,) * 4,
            scratch_shapes=[
                pltpu.VMEM((5, chunks + 1, tall, LANES), jnp.float32),
                pltpu.VMEM((3 * (STEPS + 1) * plane, LANES), jnp.float32),
                pltpu.VMEM((2, rows, LANES), jnp.float32),
                pltpu.VMEM((2, tall, LANES), jnp.float32),
                pltpu.VMEM((chunks, rows, LANES), jnp.float32),
                pltpu.VMEM((n_gy, half, 2 * GAUGE_DEV), jnp.float32),
                pltpu.VMEM((n_gy, half, 2 * GAUGE_DEV), jnp.float32),
                pltpu.VMEM((GAUGE_DEV, 3 * STEPS), jnp.float32),
                dma((5, chunks)), dma((2,)), dma((2,)), dma((2,)), dma((2,)),
                dma((2,)), dma((2,)), dma((n_gy,)), dma((n_gy,)), dma((3, chunks + 1)),
            ],
            compiler_params=pltpu.CompilerParams(collective_id=0, has_side_effects=True,
                                                 vmem_limit_bytes=40 * 1024 * 1024),
        )(surface, east_velocity, north_velocity, east_depth, north_depth, slot_gauge, slot_cell)

    block = P("gx", "gy")
    lists = P(("gx", "gy"), None)
    return jax.shard_map(shards, mesh=mesh, in_specs=(block,) * 5 + (lists,) * 2,
                         out_specs=(block,) * 3 + (lists,), check_vma=False)
```

```python
import functools

import jax
import jax.numpy as jnp
from jax import lax
from jax.experimental import pallas as pl
from jax.experimental.pallas import tpu as pltpu
from jax.sharding import PartitionSpec as P

STEPS = 16
GAUGE_DEV = 64
LANES = 128
HALO = STEPS
time_step = 0.45
MESH = pl.DeviceIdType.MESH


def kernel(
    n_gx, n_gy, eta_hbm, east_hbm, north_hbm, hx_hbm, hy_hbm, ids_hbm, cell_hbm,
    eta_out, east_out, north_out, series_out,
    wide, hist, packed, sides, final_eta, outbox, inbox, series_buf, ids_ref, cell_ref,
    load_sem, row_send, row_recv, col_send, col_recv, corner_send, corner_recv,
    mail_send, mail_recv, out_sem, list_sem,
):
    rows, cols = eta_hbm.shape
    chunks = cols // LANES
    tall = rows + 2 * HALO
    plane = (chunks + 1) * tall + 1
    a, b = lax.axis_index("gx"), lax.axis_index("gy")
    has_up, has_down = a > 0, a < n_gx - 1
    has_left, has_right = b > 0, b < n_gy - 1

    loads = []
    for f, src in enumerate((eta_hbm, east_hbm, north_hbm, hx_hbm, hy_hbm)):
        for c in range(chunks):
            copy = pltpu.make_async_copy(
                src.at[:, c * LANES:(c + 1) * LANES],
                wide.at[f, c, HALO:HALO + rows, :], load_sem.at[f, c])
            copy.start()
            loads.append(copy)
    for k, (src, dst) in enumerate(((ids_hbm, ids_ref), (cell_hbm, cell_ref))):
        copy = pltpu.make_async_copy(src, dst, list_sem.at[k])
        copy.start()
        loads.append(copy)

    zero_rows = jnp.zeros((5, chunks, HALO, LANES), jnp.float32)
    zero_side = jnp.zeros((tall, LANES), jnp.float32)
    zero_cap = jnp.zeros((2, HALO, LANES), jnp.float32)

    @pl.when(jnp.logical_not(has_up))
    def _():
        wide[:, 0:chunks, 0:HALO, :] = zero_rows
        sides[:, 0:HALO, :] = zero_cap

    @pl.when(jnp.logical_not(has_down))
    def _():
        wide[:, 0:chunks, HALO + rows:tall, :] = zero_rows
        sides[:, HALO + rows:tall, :] = zero_cap

    @pl.when(jnp.logical_not(has_left))
    def _():
        sides[0, HALO:HALO + rows, :] = zero_side[:rows]

    @pl.when(jnp.logical_not(has_right))
    def _():
        sides[1, HALO:HALO + rows, :] = zero_side[:rows]

    barrier = pltpu.get_barrier_semaphore()

    @pl.when(has_up)
    def _():
        pl.semaphore_signal(barrier, inc=1, device_id=(a - 1, b), device_id_type=MESH)

    @pl.when(has_down)
    def _():
        pl.semaphore_signal(barrier, inc=1, device_id=(a + 1, b), device_id_type=MESH)

    for d in range(1, n_gy):
        pl.semaphore_signal(barrier, inc=1, device_id=(a, lax.rem(b + d, n_gy)), device_id_type=MESH)
    pl.semaphore_wait(
        barrier, n_gy - 1 + has_up.astype(jnp.int32) + has_down.astype(jnp.int32))

    for copy in loads:
        copy.wait()

    def row_copy(k):
        source = (HALO, rows)[k]
        target = (HALO + rows, 0)[k]
        return pltpu.make_async_remote_copy(
            wide.at[:, 0:chunks, source:source + HALO, :],
            wide.at[:, 0:chunks, target:target + HALO, :],
            row_send.at[k], row_recv.at[k],
            device_id=(a + (-1, 1)[k], b), device_id_type=MESH)

    def corner_copy(k):
        source = (HALO, rows)[k]
        target = (HALO + rows, 0)[k]
        return pltpu.make_async_remote_copy(
            sides.at[:, source:source + HALO, :], sides.at[:, target:target + HALO, :],
            corner_send.at[k], corner_recv.at[k],
            device_id=(a + (-1, 1)[k], b), device_id_type=MESH)

    def col_copy(k):
        return pltpu.make_async_remote_copy(
            packed.at[k], sides.at[k, HALO:HALO + rows, :],
            col_send.at[k], col_recv.at[k],
            device_id=(a, b + (1, -1)[k]), device_id_type=MESH)

    lane = lax.broadcasted_iota(jnp.int32, (rows, LANES), 1)
    for k in range(2):
        total = jnp.zeros((rows, LANES), jnp.float32)
        for f in range(5):
            tile = wide[f, (chunks - 1, 0)[k], HALO:HALO + rows, :]
            shift = (f * HALO + (HALO, 0)[k]) % LANES
            moved = pltpu.roll(tile, shift, axis=1) if shift else tile
            total = jnp.where((lane >= f * HALO) & (lane < (f + 1) * HALO), moved, total)
        packed[k] = total

    @pl.when(has_right)
    def _():
        col_copy(0).start()

    @pl.when(has_left)
    def _():
        col_copy(1).start()

    @pl.when(has_up)
    def _():
        row_copy(0).start()

    @pl.when(has_down)
    def _():
        row_copy(1).start()

    @pl.when(has_right)
    def _():
        col_copy(0).wait_send()
        col_copy(1).wait_recv()

    @pl.when(has_left)
    def _():
        col_copy(1).wait_send()
        col_copy(0).wait_recv()

    @pl.when(has_up)
    def _():
        corner_copy(0).start()

    @pl.when(has_down)
    def _():
        corner_copy(1).start()

    @pl.when(has_up)
    def _():
        row_copy(0).wait_send()
        row_copy(1).wait_recv()
        corner_copy(0).wait_send()
        corner_copy(1).wait_recv()

    @pl.when(has_down)
    def _():
        row_copy(1).wait_send()
        row_copy(0).wait_recv()
        corner_copy(1).wait_send()
        corner_copy(0).wait_recv()

    lane = lax.broadcasted_iota(jnp.int32, (tall, LANES), 1)
    scales = (time_step, 1.0, 1.0, time_step * time_step, time_step * time_step)
    for f in range(5):
        for c in range(chunks + 1):
            if c < chunks:
                tile = wide[f, c]
            else:
                left, right = sides[0], sides[1]
                left = pltpu.roll(left, (LANES - HALO - f * HALO) % LANES, axis=1)
                if f:
                    right = pltpu.roll(right, (LANES - f * HALO) % LANES, axis=1)
                tile = jnp.where(lane < HALO, right, jnp.where(lane >= LANES - HALO, left, 0.0))
            if f in (0, 3, 4):
                tile = tile * scales[f]
            if f < 3:
                start = f * (STEPS + 1) * plane + c * tall
                hist[start:start + tall, :] = tile
            else:
                wide[f, c] = tile

    keep_row = has_down.astype(jnp.float32)
    keep_col = has_right.astype(jnp.float32)
    sub = lax.broadcasted_iota(jnp.int32, (8, LANES), 0)
    lane = lax.broadcasted_iota(jnp.int32, (8, LANES), 1)
    first_lane, last_lane = lane == 0, lane == LANES - 1
    first_sub, last_sub = sub == 0, sub == 7
    side_mask = jnp.where(lane < LANES // 2, keep_col, 1.0)
    every = range(chunks + 1)

    def step(low, high, s, carry):
        def at(f, c, t, block):
            return pl.ds((f * (STEPS + 1) + t) * plane + c * tall + block * 8, 8)

        def load_eta(block):
            tiles = [hist[at(0, c, s, block), :] for c in every]
            return tiles, [pltpu.roll(tile, 7, axis=0) for tile in tiles]

        ahead = load_eta(low)
        above = None
        for block in range(low, high):
            eta, lifted = ahead
            ahead = load_eta(block + 1) if block + 1 < high else ahead
            shifted = [pltpu.roll(tile, LANES - 1, axis=1) for tile in eta]
            lowered, moved, part = [], [], []
            for c in every:
                down = jnp.where(last_sub, ahead[1][c], lifted[c])
                right = jnp.where(last_lane, shifted[(c + 1) % (chunks + 1)], shifted[c])
                east = hist[at(1, c, s, block), :] - (down - eta[c])
                north = hist[at(2, c, s, block), :] - (right - eta[c])
                hist[at(1, c, s + 1, block), :] = east
                hist[at(2, c, s + 1, block), :] = north
                fx = wide[3, c, block * 8:block * 8 + 8] * east
                fy = wide[4, c, block * 8:block * 8 + 8] * north
                lowered.append(pltpu.roll(fx, 1, axis=0))
                moved.append(pltpu.roll(fy, 1, axis=1))
                part.append(eta[c] - fx - fy)
            if above is None:
                above = lowered
            for c in every:
                up = jnp.where(first_sub, above[c], lowered[c])
                left = jnp.where(first_lane, moved[c - 1], moved[c])
                new = part[c] + up + left
                if c == chunks:
                    new = new * side_mask
                if block * 8 >= HALO + rows:
                    new = new * keep_row
                hist[at(0, c, s + 1, block), :] = new
            above = lowered
        return carry

    blocks = tall // 8
    lax.fori_loop(0, STEPS // 2, functools.partial(step, 0, blocks), 0)
    trim = STEPS // 16
    lax.fori_loop(STEPS // 2, STEPS, functools.partial(step, trim, blocks - trim), 0)

    outs = []
    for c in range(chunks):
        start = STEPS * plane + c * tall + HALO
        final_eta[c] = hist[start:start + rows, :] * (1.0 / time_step)
        where_out = pl.ds(c * LANES, LANES)
        outs.append(pltpu.make_async_copy(final_eta.at[c], eta_out.at[:, where_out], out_sem.at[0, c]))
        for f, dst in ((1, east_out), (2, north_out)):
            start = (f * (STEPS + 1) + STEPS) * plane + c * tall + HALO
            outs.append(pltpu.make_async_copy(
                hist.at[start:start + rows, :], dst.at[:, where_out], out_sem.at[f, c]))
    for copy in outs:
        copy.start()

    slots = ids_ref.shape[1]
    slot_lane = lax.broadcasted_iota(jnp.int32, (STEPS, slots), 1)

    def pick(k, kept):
        cell = cell_ref[0, k]
        row = lax.shift_right_logical(cell, cols.bit_length() - 1)
        chunk = lax.shift_right_logical(cell, 7) & (chunks - 1)
        start = plane + chunk * tall + HALO + row
        shift = (k - cell) & (LANES - 1)
        new = []
        for f in range(3):
            slab = hist[pl.ds(f * (STEPS + 1) * plane + start, STEPS, stride=plane), :]
            slab = pltpu.roll(slab, shift, axis=1)
            new.append(jnp.where(slot_lane == k, slab, kept[f]))
        return tuple(new)

    blank = jnp.zeros((STEPS, slots), jnp.float32)
    kept = lax.fori_loop(0, slots, pick, (blank, blank, blank), unroll=8)
    records = jnp.concatenate([kept[0] * (1.0 / time_step), kept[1], kept[2]], 0)
    half = 3 * STEPS // 2
    pair = jnp.concatenate([records[:half], records[half:]], 1)
    high = pair.astype(jnp.bfloat16)
    rest = pair - high.astype(jnp.float32)
    middle = rest.astype(jnp.bfloat16)
    low = (rest - middle.astype(jnp.float32)).astype(jnp.bfloat16)
    local_ids = ids_ref[...] - a * (n_gy * GAUGE_DEV)
    entry = lax.broadcasted_iota(jnp.int32, (2 * GAUGE_DEV, slots), 0)
    for o in range(n_gy):
        lower = (entry < GAUGE_DEV) & (local_ids == entry + o * GAUGE_DEV)
        upper = (entry >= GAUGE_DEV) & (local_ids == entry + (o - 1) * GAUGE_DEV)
        chooser = jnp.concatenate(
            [jnp.where(lower, 1.0, 0.0), jnp.where(upper, 1.0, 0.0)], 1).astype(jnp.bfloat16)
        total = None
        for piece in (low, middle, high):
            got = lax.dot_general(piece, chooser, (((1,), (1,)), ((), ())),
                                  preferred_element_type=jnp.float32)
            total = got if total is None else total + got
        outbox[o] = total

    def mail(d):
        peer = lax.rem(b + d, n_gy)
        return pltpu.make_async_remote_copy(
            outbox.at[peer], inbox.at[d], mail_send.at[d], mail_recv.at[d],
            device_id=(a, peer), device_id_type=MESH)

    for d in range(1, n_gy):
        mail(d).start()
    total = outbox[b]
    for d in range(1, n_gy):
        mail(d).wait_recv()
        total = total + inbox[d]
    series_buf[0:half, :] = total[:, :GAUGE_DEV]
    series_buf[half:2 * half, :] = pltpu.roll(total, GAUGE_DEV, axis=1)[:, :GAUGE_DEV]
    last = pltpu.make_async_copy(series_buf, series_out, out_sem.at[0, chunks])
    last.start()
    for d in range(1, n_gy):
        mail(d).wait_send()
    for copy in outs:
        copy.wait()
    last.wait()


def flush(*refs):
    sem = refs[8]
    copies = [pltpu.make_async_copy(refs[k], refs[4 + k], sem.at[k]) for k in range(4)]
    for copy in copies:
        copy.start()
    for copy in copies:
        copy.wait()


def solution(mesh):
    n_gx, n_gy = mesh.shape["gx"], mesh.shape["gy"]

    def shards(surface, east_velocity, north_velocity, east_depth, north_depth, slot_gauge, slot_cell):
        rows, cols = surface.shape
        chunks = cols // LANES
        tall = rows + 2 * HALO
        plane = (chunks + 1) * tall + 1
        half = 3 * STEPS // 2
        field = jax.ShapeDtypeStruct((rows, cols), jnp.float32)
        anywhere = pl.BlockSpec(memory_space=pl.ANY)
        in_hbm = pl.BlockSpec(memory_space=pltpu.HBM)
        near = pltpu.VMEM((rows, cols), jnp.float32)
        in_vmem = pl.BlockSpec(memory_space=pltpu.VMEM)
        series = jax.ShapeDtypeStruct((3 * STEPS, GAUGE_DEV), jnp.float32)
        slots = slot_gauge.shape[1]
        dma = pltpu.SemaphoreType.DMA
        results = pl.pallas_call(
            lambda *refs: kernel(n_gx, n_gy, *refs),
            name="window",
            out_shape=(near, near, near, pltpu.VMEM(series.shape, series.dtype)),
            in_specs=[in_hbm] * 7,
            out_specs=(anywhere,) * 4,
            scratch_shapes=[
                pltpu.VMEM((5, chunks + 1, tall, LANES), jnp.float32),
                pltpu.VMEM((3 * (STEPS + 1) * plane, LANES), jnp.float32),
                pltpu.VMEM((2, rows, LANES), jnp.float32),
                pltpu.VMEM((2, tall, LANES), jnp.float32),
                pltpu.VMEM((chunks, rows, LANES), jnp.float32),
                pltpu.VMEM((n_gy, half, 2 * GAUGE_DEV), jnp.float32),
                pltpu.VMEM((n_gy, half, 2 * GAUGE_DEV), jnp.float32),
                pltpu.VMEM((3 * STEPS, GAUGE_DEV), jnp.float32),
                pltpu.VMEM((1, slots), jnp.int32), pltpu.SMEM((1, slots), jnp.int32),
                dma((5, chunks)), dma((2,)), dma((2,)), dma((2,)), dma((2,)),
                dma((2,)), dma((2,)), dma((n_gy,)), dma((n_gy,)), dma((3, chunks + 1)), dma((2,)),
            ],
            compiler_params=pltpu.CompilerParams(collective_id=0, has_side_effects=True,
                                                 vmem_limit_bytes=40 * 1024 * 1024),
        )(*[pltpu.with_memory_space_constraint(x, pltpu.HBM) for x in (
            surface, east_velocity, north_velocity, east_depth, north_depth, slot_gauge, slot_cell)])
        eta, east, north, gauges = pl.pallas_call(
            flush, name="flush", out_shape=(field, field, field, series),
            in_specs=[in_vmem] * 4, out_specs=(in_hbm,) * 4,
            scratch_shapes=[dma((4,))],
        )(*[pltpu.with_memory_space_constraint(x, pltpu.VMEM) for x in results])
        return eta, east, north, gauges.T

    block = P("gx", "gy")
    lists = P(("gx", "gy"), None)
    return jax.shard_map(shards, mesh=mesh, in_specs=(block,) * 5 + (lists,) * 2,
                         out_specs=(block,) * 3 + (lists,), check_vma=False)
```

```python
import functools

import jax
import jax.numpy as jnp
from jax import lax
from jax.experimental import pallas as pl
from jax.experimental.pallas import tpu as pltpu
from jax.sharding import PartitionSpec as P

STEPS = 16
GAUGE_DEV = 64
LANES = 128
HALO = STEPS
time_step = 0.45
MESH = pl.DeviceIdType.MESH


def kernel(
    n_gx, n_gy, eta_hbm, east_hbm, north_hbm, hx_hbm, hy_hbm, ids_hbm, cell_hbm,
    eta_out, east_out, north_out, series_out,
    wide, coef, hist, packed, sides, final_eta, outbox, inbox, series_buf, ids_ref, cell_ref,
    load_sem, row_send, row_recv, col_send, col_recv, corner_send, corner_recv,
    mail_send, mail_recv, out_sem, list_sem,
):
    rows, cols = eta_hbm.shape
    chunks = cols // LANES
    tall = rows + 2 * HALO
    plane = (chunks + 1) * tall + 1
    a, b = lax.axis_index("gx"), lax.axis_index("gy")
    has_up, has_down = a > 0, a < n_gx - 1
    has_left, has_right = b > 0, b < n_gy - 1

    loads = []
    for f, src in enumerate((eta_hbm, east_hbm, north_hbm, hx_hbm, hy_hbm)):
        for c in range(chunks):
            copy = pltpu.make_async_copy(
                src.at[:, c * LANES:(c + 1) * LANES],
                wide.at[f, c, HALO:HALO + rows, :], load_sem.at[f, c])
            copy.start()
            loads.append(copy)
    for k, (src, dst) in enumerate(((ids_hbm, ids_ref), (cell_hbm, cell_ref))):
        copy = pltpu.make_async_copy(src, dst, list_sem.at[k])
        copy.start()
        loads.append(copy)

    zero_rows = jnp.zeros((5, chunks, HALO, LANES), jnp.float32)
    zero_side = jnp.zeros((tall, LANES), jnp.float32)
    zero_cap = jnp.zeros((2, HALO, LANES), jnp.float32)

    @pl.when(jnp.logical_not(has_up))
    def _():
        wide[:, :, 0:HALO, :] = zero_rows
        sides[:, 0:HALO, :] = zero_cap

    @pl.when(jnp.logical_not(has_down))
    def _():
        wide[:, :, HALO + rows:tall, :] = zero_rows
        sides[:, HALO + rows:tall, :] = zero_cap

    @pl.when(jnp.logical_not(has_left))
    def _():
        sides[0, HALO:HALO + rows, :] = zero_side[:rows]

    @pl.when(jnp.logical_not(has_right))
    def _():
        sides[1, HALO:HALO + rows, :] = zero_side[:rows]

    barrier = pltpu.get_barrier_semaphore()

    @pl.when(has_up)
    def _():
        pl.semaphore_signal(barrier, inc=1, device_id=(a - 1, b), device_id_type=MESH)

    @pl.when(has_down)
    def _():
        pl.semaphore_signal(barrier, inc=1, device_id=(a + 1, b), device_id_type=MESH)

    for d in range(1, n_gy):
        pl.semaphore_signal(barrier, inc=1, device_id=(a, lax.rem(b + d, n_gy)), device_id_type=MESH)
    pl.semaphore_wait(
        barrier, n_gy - 1 + has_up.astype(jnp.int32) + has_down.astype(jnp.int32))

    for copy in loads:
        copy.wait()

    def row_copy(k):
        source = (HALO, rows)[k]
        target = (HALO + rows, 0)[k]
        return pltpu.make_async_remote_copy(
            wide.at[:, :, source:source + HALO, :],
            wide.at[:, :, target:target + HALO, :],
            row_send.at[k], row_recv.at[k],
            device_id=(a + (-1, 1)[k], b), device_id_type=MESH)

    def corner_copy(k):
        source = (HALO, rows)[k]
        target = (HALO + rows, 0)[k]
        return pltpu.make_async_remote_copy(
            sides.at[:, source:source + HALO, :], sides.at[:, target:target + HALO, :],
            corner_send.at[k], corner_recv.at[k],
            device_id=(a + (-1, 1)[k], b), device_id_type=MESH)

    def col_copy(k):
        return pltpu.make_async_remote_copy(
            packed.at[k], sides.at[k, HALO:HALO + rows, :],
            col_send.at[k], col_recv.at[k],
            device_id=(a, b + (1, -1)[k]), device_id_type=MESH)

    @pl.when(has_up)
    def _():
        row_copy(0).start()

    @pl.when(has_down)
    def _():
        row_copy(1).start()

    lane = lax.broadcasted_iota(jnp.int32, (rows, LANES), 1)
    for k in range(2):
        total = jnp.zeros((rows, LANES), jnp.float32)
        for f in range(5):
            tile = wide[f, (chunks - 1, 0)[k], HALO:HALO + rows, :]
            shift = (f * HALO + (HALO, 0)[k]) % LANES
            moved = pltpu.roll(tile, shift, axis=1) if shift else tile
            total = jnp.where((lane >= f * HALO) & (lane < (f + 1) * HALO), moved, total)
        packed[k] = total

    @pl.when(has_right)
    def _():
        col_copy(0).start()

    @pl.when(has_left)
    def _():
        col_copy(1).start()

    @pl.when(has_right)
    def _():
        col_copy(0).wait_send()
        col_copy(1).wait_recv()

    @pl.when(has_left)
    def _():
        col_copy(1).wait_send()
        col_copy(0).wait_recv()

    @pl.when(has_up)
    def _():
        corner_copy(0).start()

    @pl.when(has_down)
    def _():
        corner_copy(1).start()

    scales = (time_step, 1.0, 1.0, time_step * time_step, time_step * time_step)

    def prepare(low, high):
        lane = lax.broadcasted_iota(jnp.int32, (high - low, LANES), 1)
        for f in range(5):
            for c in range(chunks + 1):
                if c < chunks:
                    tile = wide[f, c, low:high]
                else:
                    left, right = sides[0, low:high], sides[1, low:high]
                    left = pltpu.roll(left, (LANES - HALO - f * HALO) % LANES, axis=1)
                    if f:
                        right = pltpu.roll(right, (LANES - f * HALO) % LANES, axis=1)
                    tile = jnp.where(lane < HALO, right, jnp.where(lane >= LANES - HALO, left, 0.0))
                if f in (0, 3, 4):
                    tile = tile * scales[f]
                if f < 3:
                    start = f * (STEPS + 1) * plane + c * tall + low
                    hist[start:start + high - low, :] = tile
                else:
                    coef[f - 3, c, low:high] = tile

    keep_row = has_down.astype(jnp.float32)
    keep_col = has_right.astype(jnp.float32)
    sub = lax.broadcasted_iota(jnp.int32, (8, LANES), 0)
    lane = lax.broadcasted_iota(jnp.int32, (8, LANES), 1)
    first_lane, last_lane = lane == 0, lane == LANES - 1
    first_sub, last_sub = sub == 0, sub == 7
    side_mask = jnp.where(lane < LANES // 2, keep_col, 1.0)
    every = range(chunks + 1)

    def sweep(s, low, high, exact_above=False, exact_ahead=False):
        def at(f, c, t, block):
            return pl.ds((f * (STEPS + 1) + t) * plane + c * tall + block * 8, 8)

        def load_eta(block):
            tiles = [hist[at(0, c, s, block), :] for c in every]
            return tiles, [pltpu.roll(tile, 7, axis=0) for tile in tiles]

        ahead = load_eta(low)
        above = None
        if exact_above:
            above = [
                pltpu.roll(coef[0, c, low * 8 - 8:low * 8] * hist[at(1, c, s + 1, low - 1), :], 1, axis=0)
                for c in every]
        for block in range(low, high):
            eta, lifted = ahead
            if block + 1 < high or exact_ahead:
                ahead = load_eta(block + 1)
            shifted = [pltpu.roll(tile, LANES - 1, axis=1) for tile in eta]
            lowered, moved, part = [], [], []
            for c in every:
                down = jnp.where(last_sub, ahead[1][c], lifted[c])
                right = jnp.where(last_lane, shifted[(c + 1) % (chunks + 1)], shifted[c])
                east = hist[at(1, c, s, block), :] - (down - eta[c])
                north = hist[at(2, c, s, block), :] - (right - eta[c])
                hist[at(1, c, s + 1, block), :] = east
                hist[at(2, c, s + 1, block), :] = north
                fx = coef[0, c, block * 8:block * 8 + 8] * east
                fy = coef[1, c, block * 8:block * 8 + 8] * north
                lowered.append(pltpu.roll(fx, 1, axis=0))
                moved.append(pltpu.roll(fy, 1, axis=1))
                part.append(eta[c] - fx - fy)
            if above is None:
                above = lowered
            for c in every:
                up = jnp.where(first_sub, above[c], lowered[c])
                left = jnp.where(first_lane, moved[c - 1], moved[c])
                new = part[c] + up + left
                if c == chunks:
                    new = new * side_mask
                if block * 8 >= HALO + rows:
                    new = new * keep_row
                hist[at(0, c, s + 1, block), :] = new
            above = lowered

    first, last = HALO // 8, (HALO + rows) // 8
    half_halo = first // 2
    middle_step = STEPS // 2

    def core_early(s, carry):
        sweep(s, first, last)
        return carry

    def core_late(s, carry):
        sweep(s, first + half_halo, last - half_halo)
        return carry

    def rim_early(s, carry):
        sweep(s, 0, first + half_halo, exact_ahead=True)
        sweep(s, last - half_halo, last + first, exact_above=True)
        return carry

    def rim_late(s, carry):
        sweep(s, half_halo, first + 2 * half_halo, exact_ahead=True)
        sweep(s, last - 2 * half_halo, last + half_halo, exact_above=True)
        return carry

    prepare(HALO, HALO + rows)
    lax.fori_loop(0, middle_step, core_early, 0)
    lax.fori_loop(middle_step, STEPS, core_late, 0)

    @pl.when(has_up)
    def _():
        row_copy(0).wait_send()
        row_copy(1).wait_recv()
        corner_copy(0).wait_send()
        corner_copy(1).wait_recv()

    @pl.when(has_down)
    def _():
        row_copy(1).wait_send()
        row_copy(0).wait_recv()
        corner_copy(1).wait_send()
        corner_copy(0).wait_recv()

    prepare(0, HALO)
    prepare(HALO + rows, tall)
    lax.fori_loop(0, middle_step, rim_early, 0)
    lax.fori_loop(middle_step, STEPS, rim_late, 0)

    outs = []
    for c in range(chunks):
        start = STEPS * plane + c * tall + HALO
        final_eta[c] = hist[start:start + rows, :] * (1.0 / time_step)
        where_out = pl.ds(c * LANES, LANES)
        outs.append(pltpu.make_async_copy(final_eta.at[c], eta_out.at[:, where_out], out_sem.at[0, c]))
        for f, dst in ((1, east_out), (2, north_out)):
            start = (f * (STEPS + 1) + STEPS) * plane + c * tall + HALO
            outs.append(pltpu.make_async_copy(
                hist.at[start:start + rows, :], dst.at[:, where_out], out_sem.at[f, c]))
    for copy in outs:
        copy.start()

    slots = ids_ref.shape[1]
    slot_lane = lax.broadcasted_iota(jnp.int32, (STEPS, slots), 1)

    def pick(k, kept):
        cell = cell_ref[0, k]
        row = lax.shift_right_logical(cell, cols.bit_length() - 1)
        chunk = lax.shift_right_logical(cell, 7) & (chunks - 1)
        start = plane + chunk * tall + HALO + row
        shift = (k - cell) & (LANES - 1)
        new = []
        for f in range(3):
            slab = hist[pl.ds(f * (STEPS + 1) * plane + start, STEPS, stride=plane), :]
            slab = pltpu.roll(slab, shift, axis=1)
            new.append(jnp.where(slot_lane == k, slab, kept[f]))
        return tuple(new)

    blank = jnp.zeros((STEPS, slots), jnp.float32)
    kept = lax.fori_loop(0, slots, pick, (blank, blank, blank), unroll=16)
    records = jnp.concatenate([kept[0] * (1.0 / time_step), kept[1], kept[2]], 0)
    half = 3 * STEPS // 2
    pair = jnp.concatenate([records[:half], records[half:]], 1)
    high = pair.astype(jnp.bfloat16)
    rest = pair - high.astype(jnp.float32)
    middle = rest.astype(jnp.bfloat16)
    low = (rest - middle.astype(jnp.float32)).astype(jnp.bfloat16)
    local_ids = ids_ref[...] - a * (n_gy * GAUGE_DEV)
    entry = lax.broadcasted_iota(jnp.int32, (2 * GAUGE_DEV, slots), 0)
    for o in range(n_gy):
        lower = (entry < GAUGE_DEV) & (local_ids == entry + o * GAUGE_DEV)
        upper = (entry >= GAUGE_DEV) & (local_ids == entry + (o - 1) * GAUGE_DEV)
        chooser = jnp.concatenate(
            [jnp.where(lower, 1.0, 0.0), jnp.where(upper, 1.0, 0.0)], 1).astype(jnp.bfloat16)
        total = None
        for piece in (low, middle, high):
            got = lax.dot_general(piece, chooser, (((1,), (1,)), ((), ())),
                                  preferred_element_type=jnp.float32)
            total = got if total is None else total + got
        outbox[o] = total

    def mail(d):
        peer = lax.rem(b + d, n_gy)
        return pltpu.make_async_remote_copy(
            outbox.at[peer], inbox.at[d], mail_send.at[d], mail_recv.at[d],
            device_id=(a, peer), device_id_type=MESH)

    for d in range(1, n_gy):
        mail(d).start()
    total = outbox[b]
    for d in range(1, n_gy):
        mail(d).wait_recv()
        total = total + inbox[d]
    series_buf[0:half, :] = total[:, :GAUGE_DEV]
    series_buf[half:2 * half, :] = pltpu.roll(total, GAUGE_DEV, axis=1)[:, :GAUGE_DEV]
    final = pltpu.make_async_copy(series_buf, series_out, out_sem.at[0, chunks])
    final.start()
    for d in range(1, n_gy):
        mail(d).wait_send()
    for copy in outs:
        copy.wait()
    final.wait()


def flush(*refs):
    sem = refs[8]
    copies = [pltpu.make_async_copy(refs[k], refs[4 + k], sem.at[k]) for k in range(4)]
    for copy in copies:
        copy.start()
    for copy in copies:
        copy.wait()


def solution(mesh):
    n_gx, n_gy = mesh.shape["gx"], mesh.shape["gy"]

    def shards(surface, east_velocity, north_velocity, east_depth, north_depth, slot_gauge, slot_cell):
        rows, cols = surface.shape
        chunks = cols // LANES
        tall = rows + 2 * HALO
        plane = (chunks + 1) * tall + 1
        half = 3 * STEPS // 2
        field = jax.ShapeDtypeStruct((rows, cols), jnp.float32)
        anywhere = pl.BlockSpec(memory_space=pl.ANY)
        in_hbm = pl.BlockSpec(memory_space=pltpu.HBM)
        near = pltpu.VMEM((rows, cols), jnp.float32)
        in_vmem = pl.BlockSpec(memory_space=pltpu.VMEM)
        series = jax.ShapeDtypeStruct((3 * STEPS, GAUGE_DEV), jnp.float32)
        slots = slot_gauge.shape[1]
        dma = pltpu.SemaphoreType.DMA
        results = pl.pallas_call(
            lambda *refs: kernel(n_gx, n_gy, *refs),
            name="window",
            out_shape=(near, near, near, pltpu.VMEM(series.shape, series.dtype)),
            in_specs=[in_hbm] * 7,
            out_specs=(anywhere,) * 4,
            scratch_shapes=[
                pltpu.VMEM((5, chunks, tall, LANES), jnp.float32),
                pltpu.VMEM((2, chunks + 1, tall, LANES), jnp.float32),
                pltpu.VMEM((3 * (STEPS + 1) * plane, LANES), jnp.float32),
                pltpu.VMEM((2, rows, LANES), jnp.float32),
                pltpu.VMEM((2, tall, LANES), jnp.float32),
                pltpu.VMEM((chunks, rows, LANES), jnp.float32),
                pltpu.VMEM((n_gy, half, 2 * GAUGE_DEV), jnp.float32),
                pltpu.VMEM((n_gy, half, 2 * GAUGE_DEV), jnp.float32),
                pltpu.VMEM((3 * STEPS, GAUGE_DEV), jnp.float32),
                pltpu.VMEM((1, slots), jnp.int32), pltpu.SMEM((1, slots), jnp.int32),
                dma((5, chunks)), dma((2,)), dma((2,)), dma((2,)), dma((2,)),
                dma((2,)), dma((2,)), dma((n_gy,)), dma((n_gy,)), dma((3, chunks + 1)), dma((2,)),
            ],
            compiler_params=pltpu.CompilerParams(collective_id=0, has_side_effects=True,
                                                 vmem_limit_bytes=40 * 1024 * 1024),
        )(*[pltpu.with_memory_space_constraint(x, pltpu.HBM) for x in (
            surface, east_velocity, north_velocity, east_depth, north_depth, slot_gauge, slot_cell)])
        eta, east, north, gauges = pl.pallas_call(
            flush, name="flush", out_shape=(field, field, field, series),
            in_specs=[in_vmem] * 4, out_specs=(in_hbm,) * 4,
            scratch_shapes=[dma((4,))],
        )(*[pltpu.with_memory_space_constraint(x, pltpu.VMEM) for x in results])
        return eta, east, north, gauges.T

    block = P("gx", "gy")
    lists = P(("gx", "gy"), None)
    return jax.shard_map(shards, mesh=mesh, in_specs=(block,) * 5 + (lists,) * 2,
                         out_specs=(block,) * 3 + (lists,), check_vma=False)
```

```python
import functools

import jax
import jax.numpy as jnp
from jax import lax
from jax.experimental import pallas as pl
from jax.experimental.pallas import tpu as pltpu
from jax.sharding import PartitionSpec as P

STEPS = 16
GAUGE_DEV = 64
LANES = 128
HALO = STEPS
time_step = 0.45
MESH = pl.DeviceIdType.MESH


def kernel(
    n_gx, n_gy, eta_hbm, east_hbm, north_hbm, hx_hbm, hy_hbm, ids_hbm, cell_hbm,
    eta_out, east_out, north_out, series_out,
    wide, coef, hist, packed, sides, final_eta, outbox, inbox, chooser, series_buf, ids_ref, cell_ref,
    load_sem, row_send, row_recv, col_send, col_recv, corner_send, corner_recv,
    mail_send, mail_recv, out_sem, list_sem,
):
    rows, cols = eta_hbm.shape
    chunks = cols // LANES
    tall = rows + 2 * HALO
    plane = (chunks + 1) * tall + 1
    a, b = lax.axis_index("gx"), lax.axis_index("gy")
    has_up, has_down = a > 0, a < n_gx - 1
    has_left, has_right = b > 0, b < n_gy - 1

    loads = []
    for f, src in enumerate((eta_hbm, east_hbm, north_hbm, hx_hbm, hy_hbm)):
        for c in range(chunks):
            copy = pltpu.make_async_copy(
                src.at[:, c * LANES:(c + 1) * LANES],
                wide.at[f, c, HALO:HALO + rows, :], load_sem.at[f, c])
            copy.start()
            loads.append(copy)
    for k, (src, dst) in enumerate(((ids_hbm, ids_ref), (cell_hbm, cell_ref))):
        copy = pltpu.make_async_copy(src, dst, list_sem.at[k])
        copy.start()
        loads.append(copy)

    zero_rows = jnp.zeros((5, chunks, HALO, LANES), jnp.float32)
    zero_side = jnp.zeros((tall, LANES), jnp.float32)
    zero_cap = jnp.zeros((2, HALO, LANES), jnp.float32)

    @pl.when(jnp.logical_not(has_up))
    def _():
        wide[:, :, 0:HALO, :] = zero_rows
        sides[:, 0:HALO, :] = zero_cap

    @pl.when(jnp.logical_not(has_down))
    def _():
        wide[:, :, HALO + rows:tall, :] = zero_rows
        sides[:, HALO + rows:tall, :] = zero_cap

    @pl.when(jnp.logical_not(has_left))
    def _():
        sides[0] = zero_side

    @pl.when(jnp.logical_not(has_right))
    def _():
        sides[1] = zero_side

    barrier = pltpu.get_barrier_semaphore()

    @pl.when(has_up)
    def _():
        pl.semaphore_signal(barrier, inc=1, device_id=(a - 1, b), device_id_type=MESH)

    @pl.when(has_down)
    def _():
        pl.semaphore_signal(barrier, inc=1, device_id=(a + 1, b), device_id_type=MESH)

    diagonals = [(v, k) for v in range(2) for k in range(2)]

    def toward(v, k):
        return jnp.logical_and((has_up, has_down)[v], (has_right, has_left)[k])

    for v, k in diagonals:
        @pl.when(toward(v, k))
        def _():
            pl.semaphore_signal(
                barrier, inc=1, device_id=(a + (-1, 1)[v], b + (1, -1)[k]), device_id_type=MESH)

    for d in range(1, n_gy):
        pl.semaphore_signal(barrier, inc=1, device_id=(a, lax.rem(b + d, n_gy)), device_id_type=MESH)
    def flag(test):
        return test.astype(jnp.int32)

    across = flag(has_up) + flag(has_down)
    pl.semaphore_wait(
        barrier, n_gy - 1 + across + across * (flag(has_left) + flag(has_right)))

    for copy in loads:
        copy.wait()

    def row_copy(k):
        source = (HALO, rows)[k]
        target = (HALO + rows, 0)[k]
        return pltpu.make_async_remote_copy(
            wide.at[:, :, source:source + HALO, :],
            wide.at[:, :, target:target + HALO, :],
            row_send.at[k], row_recv.at[k],
            device_id=(a + (-1, 1)[k], b), device_id_type=MESH)

    def corner_copy(v, k):
        source = (0, rows - HALO)[v]
        target = (HALO + rows, 0)[v]
        return pltpu.make_async_remote_copy(
            packed.at[k, source:source + HALO, :], sides.at[k, target:target + HALO, :],
            corner_send.at[v, k], corner_recv.at[v, k],
            device_id=(a + (-1, 1)[v], b + (1, -1)[k]), device_id_type=MESH)

    def col_copy(k):
        return pltpu.make_async_remote_copy(
            packed.at[k], sides.at[k, HALO:HALO + rows, :],
            col_send.at[k], col_recv.at[k],
            device_id=(a, b + (1, -1)[k]), device_id_type=MESH)

    lane = lax.broadcasted_iota(jnp.int32, (rows, LANES), 1)
    for k in range(2):
        total = jnp.zeros((rows, LANES), jnp.float32)
        for f in range(5):
            tile = wide[f, (chunks - 1, 0)[k], HALO:HALO + rows, :]
            shift = (f * HALO + (HALO, 0)[k]) % LANES
            moved = pltpu.roll(tile, shift, axis=1) if shift else tile
            total = jnp.where((lane >= f * HALO) & (lane < (f + 1) * HALO), moved, total)
        packed[k] = total

    @pl.when(has_right)
    def _():
        col_copy(0).start()

    @pl.when(has_left)
    def _():
        col_copy(1).start()

    for v, k in diagonals:
        @pl.when(toward(v, k))
        def _():
            corner_copy(v, k).start()

    @pl.when(has_up)
    def _():
        row_copy(0).start()

    @pl.when(has_down)
    def _():
        row_copy(1).start()

    @pl.when(has_right)
    def _():
        col_copy(0).wait_send()
        col_copy(1).wait_recv()

    @pl.when(has_left)
    def _():
        col_copy(1).wait_send()
        col_copy(0).wait_recv()

    scales = (time_step, 1.0, 1.0, time_step * time_step, time_step * time_step)

    def prepare(low, high):
        lane = lax.broadcasted_iota(jnp.int32, (high - low, LANES), 1)
        for f in range(5):
            for c in range(chunks + 1):
                if c < chunks:
                    tile = wide[f, c, low:high]
                else:
                    left, right = sides[0, low:high], sides[1, low:high]
                    left = pltpu.roll(left, (LANES - HALO - f * HALO) % LANES, axis=1)
                    if f:
                        right = pltpu.roll(right, (LANES - f * HALO) % LANES, axis=1)
                    tile = jnp.where(lane < HALO, right, jnp.where(lane >= LANES - HALO, left, 0.0))
                if f in (0, 3, 4):
                    tile = tile * scales[f]
                if f < 3:
                    start = f * (STEPS + 1) * plane + c * tall + low
                    hist[start:start + high - low, :] = tile
                else:
                    coef[f - 3, c, low:high] = tile

    keep_row = has_down.astype(jnp.float32)
    keep_col = has_right.astype(jnp.float32)
    sub = lax.broadcasted_iota(jnp.int32, (8, LANES), 0)
    lane = lax.broadcasted_iota(jnp.int32, (8, LANES), 1)
    first_lane, last_lane = lane == 0, lane == LANES - 1
    first_sub, last_sub = sub == 0, sub == 7
    side_mask = jnp.where(lane < LANES // 2, keep_col, 1.0)
    every = range(chunks + 1)

    def sweep(s, low, high, exact_above=False, exact_ahead=False):
        def at(f, c, t, block):
            return pl.ds((f * (STEPS + 1) + t) * plane + c * tall + block * 8, 8)

        def load_eta(block):
            tiles = [hist[at(0, c, s, block), :] for c in every]
            return tiles, [pltpu.roll(tile, 7, axis=0) for tile in tiles]

        ahead = load_eta(low)
        above = None
        if exact_above:
            above = [
                pltpu.roll(coef[0, c, low * 8 - 8:low * 8] * hist[at(1, c, s + 1, low - 1), :], 1, axis=0)
                for c in every]
        for block in range(low, high):
            eta, lifted = ahead
            if block + 1 < high or exact_ahead:
                ahead = load_eta(block + 1)
            shifted = [pltpu.roll(tile, LANES - 1, axis=1) for tile in eta]
            lowered, moved, part = [], [], []
            for c in every:
                down = jnp.where(last_sub, ahead[1][c], lifted[c])
                right = jnp.where(last_lane, shifted[(c + 1) % (chunks + 1)], shifted[c])
                east = hist[at(1, c, s, block), :] - (down - eta[c])
                north = hist[at(2, c, s, block), :] - (right - eta[c])
                hist[at(1, c, s + 1, block), :] = east
                hist[at(2, c, s + 1, block), :] = north
                fx = coef[0, c, block * 8:block * 8 + 8] * east
                fy = coef[1, c, block * 8:block * 8 + 8] * north
                lowered.append(pltpu.roll(fx, 1, axis=0))
                moved.append(pltpu.roll(fy, 1, axis=1))
                part.append(eta[c] - fx - fy)
            if above is None:
                above = lowered
            for c in every:
                up = jnp.where(first_sub, above[c], lowered[c])
                left = jnp.where(first_lane, moved[c - 1], moved[c])
                new = part[c] + up + left
                if c == chunks:
                    new = new * side_mask
                if block * 8 >= HALO + rows:
                    new = new * keep_row
                hist[at(0, c, s + 1, block), :] = new
            above = lowered

    first, last = HALO // 8, (HALO + rows) // 8
    half_halo = first // 2
    middle_step = STEPS // 2

    def core_early(s, carry):
        sweep(s, first, last)
        return carry

    def core_late(s, carry):
        sweep(s, first + half_halo, last - half_halo)
        return carry

    def rim_early(s, carry):
        sweep(s, 0, first + half_halo, exact_ahead=True)
        sweep(s, last - half_halo, last + first, exact_above=True)
        return carry

    def rim_late(s, carry):
        sweep(s, half_halo, first + 2 * half_halo, exact_ahead=True)
        sweep(s, last - 2 * half_halo, last + half_halo, exact_above=True)
        return carry

    prepare(HALO, HALO + rows)
    lax.fori_loop(0, middle_step, core_early, 0)
    lax.fori_loop(middle_step, STEPS, core_late, 0)

    slots = ids_ref.shape[1]
    local_ids = ids_ref[...] - a * (n_gy * GAUGE_DEV)
    entry = lax.broadcasted_iota(jnp.int32, (2 * GAUGE_DEV, slots), 0)
    for o in range(n_gy):
        lower = (entry < GAUGE_DEV) & (local_ids == entry + o * GAUGE_DEV)
        upper = (entry >= GAUGE_DEV) & (local_ids == entry + (o - 1) * GAUGE_DEV)
        chooser[o] = jnp.concatenate(
            [jnp.where(lower, 1.0, 0.0), jnp.where(upper, 1.0, 0.0)], 1).astype(jnp.bfloat16)

    @pl.when(has_up)
    def _():
        row_copy(0).wait_send()
        row_copy(1).wait_recv()

    @pl.when(has_down)
    def _():
        row_copy(1).wait_send()
        row_copy(0).wait_recv()

    for v, k in diagonals:
        @pl.when(toward(v, k))
        def _():
            corner_copy(v, k).wait_send()
            corner_copy(1 - v, 1 - k).wait_recv()

    prepare(0, HALO)
    prepare(HALO + rows, tall)
    lax.fori_loop(0, middle_step, rim_early, 0)
    lax.fori_loop(middle_step, STEPS, rim_late, 0)

    slot_lane = lax.broadcasted_iota(jnp.int32, (STEPS, slots), 1)

    def pick(k, kept):
        cell = cell_ref[0, k]
        row = lax.shift_right_logical(cell, cols.bit_length() - 1)
        chunk = lax.shift_right_logical(cell, 7) & (chunks - 1)
        start = plane + chunk * tall + HALO + row
        shift = (k - cell) & (LANES - 1)
        new = []
        for f in range(3):
            slab = hist[pl.ds(f * (STEPS + 1) * plane + start, STEPS, stride=plane), :]
            slab = pltpu.roll(slab, shift, axis=1)
            new.append(jnp.where(slot_lane == k, slab, kept[f]))
        return tuple(new)

    blank = jnp.zeros((STEPS, slots), jnp.float32)
    kept = lax.fori_loop(0, slots, pick, (blank, blank, blank), unroll=16)
    records = jnp.concatenate([kept[0] * (1.0 / time_step), kept[1], kept[2]], 0)
    half = 3 * STEPS // 2
    pair = jnp.concatenate([records[:half], records[half:]], 1)
    high = pair.astype(jnp.bfloat16)
    rest = pair - high.astype(jnp.float32)
    middle = rest.astype(jnp.bfloat16)
    low = (rest - middle.astype(jnp.float32)).astype(jnp.bfloat16)
    for o in range(n_gy):
        total = None
        for piece in (low, middle, high):
            got = lax.dot_general(piece, chooser[o], (((1,), (1,)), ((), ())),
                                  preferred_element_type=jnp.float32)
            total = got if total is None else total + got
        outbox[o] = total

    def mail(d):
        peer = lax.rem(b + d, n_gy)
        return pltpu.make_async_remote_copy(
            outbox.at[peer], inbox.at[d], mail_send.at[d], mail_recv.at[d],
            device_id=(a, peer), device_id_type=MESH)

    for d in range(1, n_gy):
        mail(d).start()

    outs = []
    for c in range(chunks):
        start = STEPS * plane + c * tall + HALO
        final_eta[c] = hist[start:start + rows, :] * (1.0 / time_step)
        where_out = pl.ds(c * LANES, LANES)
        outs.append(pltpu.make_async_copy(final_eta.at[c], eta_out.at[:, where_out], out_sem.at[0, c]))
        for f, dst in ((1, east_out), (2, north_out)):
            start = (f * (STEPS + 1) + STEPS) * plane + c * tall + HALO
            outs.append(pltpu.make_async_copy(
                hist.at[start:start + rows, :], dst.at[:, where_out], out_sem.at[f, c]))
    for copy in outs:
        copy.start()

    total = outbox[b]
    for d in range(1, n_gy):
        mail(d).wait_recv()
        total = total + inbox[d]
    series_buf[0:half, :] = total[:, :GAUGE_DEV]
    series_buf[half:2 * half, :] = pltpu.roll(total, GAUGE_DEV, axis=1)[:, :GAUGE_DEV]
    final = pltpu.make_async_copy(series_buf, series_out, out_sem.at[0, chunks])
    final.start()
    for d in range(1, n_gy):
        mail(d).wait_send()
    for copy in outs:
        copy.wait()
    final.wait()


def flush(*refs):
    sem = refs[8]
    copies = [pltpu.make_async_copy(refs[k], refs[4 + k], sem.at[k]) for k in range(4)]
    for copy in copies:
        copy.start()
    for copy in copies:
        copy.wait()


def solution(mesh):
    n_gx, n_gy = mesh.shape["gx"], mesh.shape["gy"]

    def shards(surface, east_velocity, north_velocity, east_depth, north_depth, slot_gauge, slot_cell):
        rows, cols = surface.shape
        chunks = cols // LANES
        tall = rows + 2 * HALO
        plane = (chunks + 1) * tall + 1
        half = 3 * STEPS // 2
        field = jax.ShapeDtypeStruct((rows, cols), jnp.float32)
        anywhere = pl.BlockSpec(memory_space=pl.ANY)
        in_hbm = pl.BlockSpec(memory_space=pltpu.HBM)
        near = pltpu.VMEM((rows, cols), jnp.float32)
        in_vmem = pl.BlockSpec(memory_space=pltpu.VMEM)
        series = jax.ShapeDtypeStruct((3 * STEPS, GAUGE_DEV), jnp.float32)
        slots = slot_gauge.shape[1]
        dma = pltpu.SemaphoreType.DMA
        results = pl.pallas_call(
            lambda *refs: kernel(n_gx, n_gy, *refs),
            name="window",
            out_shape=(near, near, near, pltpu.VMEM(series.shape, series.dtype)),
            in_specs=[in_hbm] * 7,
            out_specs=(anywhere,) * 4,
            scratch_shapes=[
                pltpu.VMEM((5, chunks, tall, LANES), jnp.float32),
                pltpu.VMEM((2, chunks + 1, tall, LANES), jnp.float32),
                pltpu.VMEM((3 * (STEPS + 1) * plane, LANES), jnp.float32),
                pltpu.VMEM((2, rows, LANES), jnp.float32),
                pltpu.VMEM((2, tall, LANES), jnp.float32),
                pltpu.VMEM((chunks, rows, LANES), jnp.float32),
                pltpu.VMEM((n_gy, half, 2 * GAUGE_DEV), jnp.float32),
                pltpu.VMEM((n_gy, half, 2 * GAUGE_DEV), jnp.float32),
                pltpu.VMEM((n_gy, 2 * GAUGE_DEV, 2 * slots), jnp.bfloat16),
                pltpu.VMEM((3 * STEPS, GAUGE_DEV), jnp.float32),
                pltpu.VMEM((1, slots), jnp.int32), pltpu.SMEM((1, slots), jnp.int32),
                dma((5, chunks)), dma((2,)), dma((2,)), dma((2,)), dma((2,)),
                dma((2, 2)), dma((2, 2)), dma((n_gy,)), dma((n_gy,)), dma((3, chunks + 1)), dma((2,)),
            ],
            compiler_params=pltpu.CompilerParams(collective_id=0, has_side_effects=True,
                                                 vmem_limit_bytes=40 * 1024 * 1024),
        )(*[pltpu.with_memory_space_constraint(x, pltpu.HBM) for x in (
            surface, east_velocity, north_velocity, east_depth, north_depth, slot_gauge, slot_cell)])
        eta, east, north, gauges = pl.pallas_call(
            flush, name="flush", out_shape=(field, field, field, series),
            in_specs=[in_vmem] * 4, out_specs=(in_hbm,) * 4,
            scratch_shapes=[dma((4,))],
        )(*[pltpu.with_memory_space_constraint(x, pltpu.VMEM) for x in results])
        return eta, east, north, gauges.T

    block = P("gx", "gy")
    lists = P(("gx", "gy"), None)
    return jax.shard_map(shards, mesh=mesh, in_specs=(block,) * 5 + (lists,) * 2,
                         out_specs=(block,) * 3 + (lists,), check_vma=False)
```

```python
import functools

import jax
import jax.numpy as jnp
from jax import lax
from jax.experimental import pallas as pl
from jax.experimental.pallas import tpu as pltpu
from jax.sharding import PartitionSpec as P

STEPS = 16
GAUGE_DEV = 64
LANES = 128
HALO = STEPS
time_step = 0.45
MESH = pl.DeviceIdType.MESH


def kernel(
    n_gx, n_gy, eta_hbm, east_hbm, north_hbm, hx_hbm, hy_hbm, ids_hbm, cell_hbm,
    eta_out, east_out, north_out, series_out,
    wide, coef, hist, packed, sides, final_eta, outbox, inbox, chooser, series_buf, ids_ref, cell_ref,
    load_sem, row_send, row_recv, col_send, col_recv, corner_send, corner_recv,
    mail_send, mail_recv, out_sem, list_sem,
):
    rows, cols = eta_hbm.shape
    chunks = cols // LANES
    tall = rows + 2 * HALO
    plane = (chunks + 1) * tall + 1
    a, b = lax.axis_index("gx"), lax.axis_index("gy")
    has_up, has_down = a > 0, a < n_gx - 1
    has_left, has_right = b > 0, b < n_gy - 1

    loads = []
    for f, src in enumerate((eta_hbm, east_hbm, north_hbm, hx_hbm, hy_hbm)):
        for c in range(chunks):
            copy = pltpu.make_async_copy(
                src.at[:, c * LANES:(c + 1) * LANES],
                wide.at[f, c, HALO:HALO + rows, :], load_sem.at[f, c])
            copy.start()
            loads.append(copy)
    for k, (src, dst) in enumerate(((ids_hbm, ids_ref), (cell_hbm, cell_ref))):
        copy = pltpu.make_async_copy(src, dst, list_sem.at[k])
        copy.start()
        loads.append(copy)

    zero_rows = jnp.zeros((5, chunks, HALO, LANES), jnp.float32)
    zero_side = jnp.zeros((tall, LANES), jnp.float32)
    zero_cap = jnp.zeros((2, HALO, LANES), jnp.float32)

    @pl.when(jnp.logical_not(has_up))
    def _():
        wide[:, :, 0:HALO, :] = zero_rows
        sides[:, 0:HALO, :] = zero_cap

    @pl.when(jnp.logical_not(has_down))
    def _():
        wide[:, :, HALO + rows:tall, :] = zero_rows
        sides[:, HALO + rows:tall, :] = zero_cap

    @pl.when(jnp.logical_not(has_left))
    def _():
        sides[0] = zero_side

    @pl.when(jnp.logical_not(has_right))
    def _():
        sides[1] = zero_side

    barrier = pltpu.get_barrier_semaphore()

    @pl.when(has_up)
    def _():
        pl.semaphore_signal(barrier, inc=1, device_id=(a - 1, b), device_id_type=MESH)

    @pl.when(has_down)
    def _():
        pl.semaphore_signal(barrier, inc=1, device_id=(a + 1, b), device_id_type=MESH)

    diagonals = [(v, k) for v in range(2) for k in range(2)]

    def toward(v, k):
        return jnp.logical_and((has_up, has_down)[v], (has_right, has_left)[k])

    for v, k in diagonals:
        @pl.when(toward(v, k))
        def _():
            pl.semaphore_signal(
                barrier, inc=1, device_id=(a + (-1, 1)[v], b + (1, -1)[k]), device_id_type=MESH)

    for d in range(1, n_gy):
        pl.semaphore_signal(barrier, inc=1, device_id=(a, lax.rem(b + d, n_gy)), device_id_type=MESH)
    def flag(test):
        return test.astype(jnp.int32)

    across = flag(has_up) + flag(has_down)
    pl.semaphore_wait(
        barrier, n_gy - 1 + across + across * (flag(has_left) + flag(has_right)))

    for copy in loads:
        copy.wait()

    near = HALO // 2

    def row_copy(k, part):
        shift = near * (part if k == 0 else 1 - part)
        source = (HALO, rows)[k] + shift
        target = (HALO + rows, 0)[k] + shift
        return pltpu.make_async_remote_copy(
            wide.at[:, :, source:source + near, :],
            wide.at[:, :, target:target + near, :],
            row_send.at[k, part], row_recv.at[k, part],
            device_id=(a + (-1, 1)[k], b), device_id_type=MESH)

    def corner_copy(v, k):
        source = (0, rows - HALO)[v]
        target = (HALO + rows, 0)[v]
        return pltpu.make_async_remote_copy(
            packed.at[k, source:source + HALO, :], sides.at[k, target:target + HALO, :],
            corner_send.at[v, k], corner_recv.at[v, k],
            device_id=(a + (-1, 1)[v], b + (1, -1)[k]), device_id_type=MESH)

    def col_copy(k):
        return pltpu.make_async_remote_copy(
            packed.at[k], sides.at[k, HALO:HALO + rows, :],
            col_send.at[k], col_recv.at[k],
            device_id=(a, b + (1, -1)[k]), device_id_type=MESH)

    lane = lax.broadcasted_iota(jnp.int32, (rows, LANES), 1)
    for k in range(2):
        total = jnp.zeros((rows, LANES), jnp.float32)
        for f in range(5):
            tile = wide[f, (chunks - 1, 0)[k], HALO:HALO + rows, :]
            shift = (f * HALO + (HALO, 0)[k]) % LANES
            moved = pltpu.roll(tile, shift, axis=1) if shift else tile
            total = jnp.where((lane >= f * HALO) & (lane < (f + 1) * HALO), moved, total)
        packed[k] = total

    @pl.when(has_right)
    def _():
        col_copy(0).start()

    @pl.when(has_left)
    def _():
        col_copy(1).start()

    for v, k in diagonals:
        @pl.when(toward(v, k))
        def _():
            corner_copy(v, k).start()

    @pl.when(has_up)
    def _():
        row_copy(0, 0).start()
        row_copy(0, 1).start()

    @pl.when(has_down)
    def _():
        row_copy(1, 0).start()
        row_copy(1, 1).start()

    @pl.when(has_right)
    def _():
        col_copy(0).wait_send()
        col_copy(1).wait_recv()

    @pl.when(has_left)
    def _():
        col_copy(1).wait_send()
        col_copy(0).wait_recv()

    scales = (time_step, 1.0, 1.0, time_step * time_step, time_step * time_step)

    def prepare(low, high):
        lane = lax.broadcasted_iota(jnp.int32, (high - low, LANES), 1)
        for f in range(5):
            for c in range(chunks + 1):
                if c < chunks:
                    tile = wide[f, c, low:high]
                else:
                    left, right = sides[0, low:high], sides[1, low:high]
                    left = pltpu.roll(left, (LANES - HALO - f * HALO) % LANES, axis=1)
                    if f:
                        right = pltpu.roll(right, (LANES - f * HALO) % LANES, axis=1)
                    tile = jnp.where(lane < HALO, right, jnp.where(lane >= LANES - HALO, left, 0.0))
                if f in (0, 3, 4):
                    tile = tile * scales[f]
                if f < 3:
                    start = f * (STEPS + 1) * plane + c * tall + low
                    hist[start:start + high - low, :] = tile
                else:
                    coef[f - 3, c, low:high] = tile

    keep_row = has_down.astype(jnp.float32)
    keep_col = has_right.astype(jnp.float32)
    sub = lax.broadcasted_iota(jnp.int32, (8, LANES), 0)
    lane = lax.broadcasted_iota(jnp.int32, (8, LANES), 1)
    first_lane, last_lane = lane == 0, lane == LANES - 1
    first_sub, last_sub = sub == 0, sub == 7
    side_mask = jnp.where(lane < LANES // 2, keep_col, 1.0)
    every = range(chunks + 1)

    def sweep(s, low, high, exact_above=False, exact_ahead=False):
        def at(f, c, t, block):
            return pl.ds((f * (STEPS + 1) + t) * plane + c * tall + block * 8, 8)

        def load_eta(block):
            tiles = [hist[at(0, c, s, block), :] for c in every]
            return tiles, [pltpu.roll(tile, 7, axis=0) for tile in tiles]

        ahead = load_eta(low)
        above = None
        if exact_above:
            above = [
                pltpu.roll(coef[0, c, low * 8 - 8:low * 8] * hist[at(1, c, s + 1, low - 1), :], 1, axis=0)
                for c in every]
        for block in range(low, high):
            eta, lifted = ahead
            if block + 1 < high or exact_ahead:
                ahead = load_eta(block + 1)
            shifted = [pltpu.roll(tile, LANES - 1, axis=1) for tile in eta]
            lowered, moved, part = [], [], []
            for c in every:
                down = jnp.where(last_sub, ahead[1][c], lifted[c])
                right = jnp.where(last_lane, shifted[(c + 1) % (chunks + 1)], shifted[c])
                east = hist[at(1, c, s, block), :] - (down - eta[c])
                north = hist[at(2, c, s, block), :] - (right - eta[c])
                hist[at(1, c, s + 1, block), :] = east
                hist[at(2, c, s + 1, block), :] = north
                fx = coef[0, c, block * 8:block * 8 + 8] * east
                fy = coef[1, c, block * 8:block * 8 + 8] * north
                lowered.append(pltpu.roll(fx, 1, axis=0))
                moved.append(pltpu.roll(fy, 1, axis=1))
                part.append(eta[c] - fx - fy)
            if above is None:
                above = lowered
            for c in every:
                up = jnp.where(first_sub, above[c], lowered[c])
                left = jnp.where(first_lane, moved[c - 1], moved[c])
                new = part[c] + up + left
                if c == chunks:
                    new = new * side_mask
                if block * 8 >= HALO + rows:
                    new = new * keep_row
                hist[at(0, c, s + 1, block), :] = new
            above = lowered

    first, last = HALO // 8, (HALO + rows) // 8
    half_halo = first // 2
    middle_step = STEPS // 2

    def core_early(s, carry):
        sweep(s, first, last)
        return carry

    def core_late(s, carry):
        sweep(s, first + half_halo, last - half_halo)
        return carry

    def rim_inner(s, carry):
        sweep(s, half_halo, first + half_halo, exact_ahead=True)
        sweep(s, last - half_halo, last + half_halo, exact_above=True)
        return carry

    def rim_outer(s, carry):
        sweep(s, 0, first, exact_ahead=True)
        sweep(s, last, last + first, exact_above=True)
        return carry

    def rim_late(s, carry):
        sweep(s, half_halo, first + 2 * half_halo, exact_ahead=True)
        sweep(s, last - 2 * half_halo, last + half_halo, exact_above=True)
        return carry

    prepare(HALO, HALO + rows)
    lax.fori_loop(0, middle_step, core_early, 0)
    lax.fori_loop(middle_step, STEPS, core_late, 0)

    slots = ids_ref.shape[1]
    local_ids = ids_ref[...] - a * (n_gy * GAUGE_DEV)
    entry = lax.broadcasted_iota(jnp.int32, (2 * GAUGE_DEV, slots), 0)
    for o in range(n_gy):
        lower = (entry < GAUGE_DEV) & (local_ids == entry + o * GAUGE_DEV)
        upper = (entry >= GAUGE_DEV) & (local_ids == entry + (o - 1) * GAUGE_DEV)
        chooser[o] = jnp.concatenate(
            [jnp.where(lower, 1.0, 0.0), jnp.where(upper, 1.0, 0.0)], 1).astype(jnp.bfloat16)

    def wait_rows(part):
        @pl.when(has_up)
        def _():
            row_copy(0, part).wait_send()
            row_copy(1, part).wait_recv()

        @pl.when(has_down)
        def _():
            row_copy(1, part).wait_send()
            row_copy(0, part).wait_recv()

    wait_rows(0)
    for v, k in diagonals:
        @pl.when(toward(v, k))
        def _():
            corner_copy(v, k).wait_send()
            corner_copy(1 - v, 1 - k).wait_recv()

    prepare(near, HALO)
    prepare(HALO + rows, HALO + rows + near)
    lax.fori_loop(0, middle_step, rim_inner, 0)
    wait_rows(1)
    prepare(0, near)
    prepare(HALO + rows + near, tall)
    lax.fori_loop(0, middle_step, rim_outer, 0)
    lax.fori_loop(middle_step, STEPS, rim_late, 0)

    slot_lane = lax.broadcasted_iota(jnp.int32, (STEPS, slots), 1)

    def pick(k, kept):
        cell = cell_ref[0, k]
        row = lax.shift_right_logical(cell, cols.bit_length() - 1)
        chunk = lax.shift_right_logical(cell, 7) & (chunks - 1)
        start = plane + chunk * tall + HALO + row
        shift = (k - cell) & (LANES - 1)
        new = []
        for f in range(3):
            slab = hist[pl.ds(f * (STEPS + 1) * plane + start, STEPS, stride=plane), :]
            slab = pltpu.roll(slab, shift, axis=1)
            new.append(jnp.where(slot_lane == k, slab, kept[f]))
        return tuple(new)

    blank = jnp.zeros((STEPS, slots), jnp.float32)
    kept = lax.fori_loop(0, slots, pick, (blank, blank, blank), unroll=16)
    records = jnp.concatenate([kept[0] * (1.0 / time_step), kept[1], kept[2]], 0)
    half = 3 * STEPS // 2
    pair = jnp.concatenate([records[:half], records[half:]], 1)
    high = pair.astype(jnp.bfloat16)
    rest = pair - high.astype(jnp.float32)
    middle = rest.astype(jnp.bfloat16)
    low = (rest - middle.astype(jnp.float32)).astype(jnp.bfloat16)
    for o in range(n_gy):
        total = None
        for piece in (low, middle, high):
            got = lax.dot_general(piece, chooser[o], (((1,), (1,)), ((), ())),
                                  preferred_element_type=jnp.float32)
            total = got if total is None else total + got
        outbox[o] = total

    def mail(d):
        peer = lax.rem(b + d, n_gy)
        return pltpu.make_async_remote_copy(
            outbox.at[peer], inbox.at[d], mail_send.at[d], mail_recv.at[d],
            device_id=(a, peer), device_id_type=MESH)

    for d in range(1, n_gy):
        mail(d).start()

    outs = []
    for c in range(chunks):
        start = STEPS * plane + c * tall + HALO
        final_eta[c] = hist[start:start + rows, :] * (1.0 / time_step)
        where_out = pl.ds(c * LANES, LANES)
        outs.append(pltpu.make_async_copy(final_eta.at[c], eta_out.at[:, where_out], out_sem.at[0, c]))
        for f, dst in ((1, east_out), (2, north_out)):
            start = (f * (STEPS + 1) + STEPS) * plane + c * tall + HALO
            outs.append(pltpu.make_async_copy(
                hist.at[start:start + rows, :], dst.at[:, where_out], out_sem.at[f, c]))
    for copy in outs:
        copy.start()

    total = outbox[b]
    for d in range(1, n_gy):
        mail(d).wait_recv()
        total = total + inbox[d]
    series_buf[0:half, :] = total[:, :GAUGE_DEV]
    series_buf[half:2 * half, :] = pltpu.roll(total, GAUGE_DEV, axis=1)[:, :GAUGE_DEV]
    final = pltpu.make_async_copy(series_buf, series_out, out_sem.at[0, chunks])
    final.start()
    for d in range(1, n_gy):
        mail(d).wait_send()
    for copy in outs:
        copy.wait()
    final.wait()


def flush(*refs):
    sem = refs[8]
    copies = [pltpu.make_async_copy(refs[k], refs[4 + k], sem.at[k]) for k in range(4)]
    for copy in copies:
        copy.start()
    for copy in copies:
        copy.wait()


def solution(mesh):
    n_gx, n_gy = mesh.shape["gx"], mesh.shape["gy"]

    def shards(surface, east_velocity, north_velocity, east_depth, north_depth, slot_gauge, slot_cell):
        rows, cols = surface.shape
        chunks = cols // LANES
        tall = rows + 2 * HALO
        plane = (chunks + 1) * tall + 1
        half = 3 * STEPS // 2
        field = jax.ShapeDtypeStruct((rows, cols), jnp.float32)
        anywhere = pl.BlockSpec(memory_space=pl.ANY)
        in_hbm = pl.BlockSpec(memory_space=pltpu.HBM)
        near = pltpu.VMEM((rows, cols), jnp.float32)
        in_vmem = pl.BlockSpec(memory_space=pltpu.VMEM)
        series = jax.ShapeDtypeStruct((3 * STEPS, GAUGE_DEV), jnp.float32)
        slots = slot_gauge.shape[1]
        dma = pltpu.SemaphoreType.DMA
        results = pl.pallas_call(
            lambda *refs: kernel(n_gx, n_gy, *refs),
            name="window",
            out_shape=(near, near, near, pltpu.VMEM(series.shape, series.dtype)),
            in_specs=[in_hbm] * 7,
            out_specs=(anywhere,) * 4,
            scratch_shapes=[
                pltpu.VMEM((5, chunks, tall, LANES), jnp.float32),
                pltpu.VMEM((2, chunks + 1, tall, LANES), jnp.float32),
                pltpu.VMEM((3 * (STEPS + 1) * plane, LANES), jnp.float32),
                pltpu.VMEM((2, rows, LANES), jnp.float32),
                pltpu.VMEM((2, tall, LANES), jnp.float32),
                pltpu.VMEM((chunks, rows, LANES), jnp.float32),
                pltpu.VMEM((n_gy, half, 2 * GAUGE_DEV), jnp.float32),
                pltpu.VMEM((n_gy, half, 2 * GAUGE_DEV), jnp.float32),
                pltpu.VMEM((n_gy, 2 * GAUGE_DEV, 2 * slots), jnp.bfloat16),
                pltpu.VMEM((3 * STEPS, GAUGE_DEV), jnp.float32),
                pltpu.VMEM((1, slots), jnp.int32), pltpu.SMEM((1, slots), jnp.int32),
                dma((5, chunks)), dma((2, 2)), dma((2, 2)), dma((2,)), dma((2,)),
                dma((2, 2)), dma((2, 2)), dma((n_gy,)), dma((n_gy,)), dma((3, chunks + 1)), dma((2,)),
            ],
            compiler_params=pltpu.CompilerParams(collective_id=0, has_side_effects=True,
                                                 vmem_limit_bytes=40 * 1024 * 1024),
        )(*[pltpu.with_memory_space_constraint(x, pltpu.HBM) for x in (
            surface, east_velocity, north_velocity, east_depth, north_depth, slot_gauge, slot_cell)])
        eta, east, north, gauges = pl.pallas_call(
            flush, name="flush", out_shape=(field, field, field, series),
            in_specs=[in_vmem] * 4, out_specs=(in_hbm,) * 4,
            scratch_shapes=[dma((4,))],
        )(*[pltpu.with_memory_space_constraint(x, pltpu.VMEM) for x in results])
        return eta, east, north, gauges.T

    block = P("gx", "gy")
    lists = P(("gx", "gy"), None)
    return jax.shard_map(shards, mesh=mesh, in_specs=(block,) * 5 + (lists,) * 2,
                         out_specs=(block,) * 3 + (lists,), check_vma=False)
```
